32 devices in a mesh: req: 8 (over z, x), head: 4 (over y, core).
Axes of the slice: x: 2, y: 2, z: 4, core: 2. Of those that a mesh axis runs over, the one named last changes fastest.
Arguments:
- hidden_in: bfloat16 [64, 2048], P('req'), may hold values from -4 to 4
- queries: bfloat16 [64, 2048], P('req', 'head'), may hold values from -7.5 to 7.5
- new_keys: bfloat16 [64, 2048], P('req', 'head'), may hold values from -10 to 10
- new_values: bfloat16 [64, 2048], P('req', 'head'), may hold values from -8 to 8
- key_cache: bfloat16 [64, 1024, 2048], P('req', None, 'head'), may hold values from -4 to 4
- value_cache: bfloat16 [64, 1024, 2048], P('req', None, 'head'), may hold values from -6 to 6
- lengths: int32 [64], P('req'), may hold values from 2 to 1024, as said below
- out_proj: bfloat16 [2048, 2048], P('head'), may hold values from -0.5 to 0.5
- norm_gain: float32 [2048], replicated, may hold values from 0.1 to 1.9
- shared_gate: bfloat16 [5632, 2048], P(('req', 'head')), may hold values from -0.125 to 0.125
- shared_up: bfloat16 [5632, 2048], P(('req', 'head')), may hold values from -0.125 to 0.125
- shared_down: bfloat16 [5632, 2048], P(('req', 'head')), may hold values from -0.078125 to 0.078125
- shared_score: float32 [2048], replicated, may hold values from -0.125 to 0.125
- expert_gate: bfloat16 [8, 2048, 1408], P('req', None, 'head'), may hold values from -0.125 to 0.125
- expert_up: bfloat16 [8, 2048, 1408], P('req', None, 'head'), may hold values from -0.125 to 0.125
- expert_down: bfloat16 [8, 1408, 2048], P('req', 'head'), may hold values from -0.15625 to 0.15625
- expert_ids: int32 [64, 4], P('req'), may hold values from 0 to 7, all different within a row; in each aligned block of 8 rows (0 to 7, 8 to 15, ...) at most 8 rows name the same one
- route_weight: bfloat16 [64, 4], P('req'), may hold values from 0.099609375 to 0.59765625
Outputs:
- layer_out: bfloat16 [64, 2048], P('req')
The draws below stay inside these ranges and needn't reach their ends.
Inputs may be any that keep to these rules, and one draw needn't show every extreme that they name: The first lengths[t] cache positions of request t are live; some request has exactly 1024. `expert_ids`: each row names 4 different experts. Among the 8 rows of one device (aligned blocks) no expert is named by more than 8 rows, and in some blocks one is named by exactly 8.
All inputs are finite; a program needn't handle non-finite values.
Results may differ from the reference program's by a relative error of at most 0.017.
Values may be sent and summed in bfloat16 or wider, within the bound.
A program may use at most 128 MiB of HBM per device.

```python
import math
import jax
import jax.numpy as jnp
import numpy as np
from jax import lax

D = 2048
HEADS = 16
HD = 128
EFF = 1408
SH = 5632
TOPK = 4
B_DEV = 8
MAXLEN = 1024
EXPERTS = 8
TOKENS = 64
CAP = 8


def draw_queries(key, part):
    first_key = jax.random.fold_in(key, 1)
    shape_full = (TOKENS, HEADS * HD)
    return jnp.clip(jax.random.normal(first_key, shape_full, jnp.float32), -4.0, 4.0).astype(jnp.bfloat16)


def draw_key_cache(key, part):
    second_key = jax.random.fold_in(key, 2)
    shape_full = (TOKENS, MAXLEN, HEADS * HD)
    return jnp.clip(jax.random.normal(second_key, shape_full, jnp.float32), -4.0, 4.0).astype(jnp.bfloat16)


def draw_lengths(key, part):
    first_key = jax.random.fold_in(key, 21)
    second_key = jax.random.fold_in(key, 22)
    third_key = jax.random.fold_in(key, 23)
    left = jax.random.randint(first_key, (TOKENS,), 1, MAXLEN + 1, dtype=jnp.int32)
    right = jax.random.randint(second_key, (TOKENS,), 1, MAXLEN + 1, dtype=jnp.int32)
    spans = jnp.maximum(left * right // MAXLEN, 2)
    chosen = jax.random.randint(third_key, (), 0, TOKENS, dtype=jnp.int32)
    return jnp.where(jnp.arange(TOKENS, dtype=jnp.int32) == chosen, MAXLEN, spans).astype(jnp.int32)


def levels(stream_key, shape, shards, least, high):
    def one(dim, parts):
        heights = jax.random.uniform(jax.random.fold_in(jax.random.fold_in(stream_key, 6), dim), (parts,), jnp.float32, least / len(shards), high / len(shards))
        return jnp.repeat(jnp.exp(heights), shape[dim] // parts).reshape((-1,) + (1,) * (len(shape) - dim - 1))

    level = one(*shards[0])
    for cut in shards[1:]:
        level = level * one(*cut)
    return level


def deal_out(stream_key, own, number, rows, count, top, most, skew):
    ranking = jax.random.permutation(stream_key, count)
    packed, ordinary = portions_of(count, rows * top, most, skew, True), portions_of(count, rows * top, most, skew, False)
    places = jnp.arange(count)

    def named(sizes, turn):
        used = int((sizes > 0).sum())
        fixed = max(1, used // 4)
        shifted = fixed + (places - fixed + turn * (used - fixed)) % max(1, count - fixed)
        return jnp.zeros((count,), jnp.int32).at[ranking[jnp.where(places < fixed, places, shifted)]].set(jnp.asarray(sizes, jnp.int32))

    sizes = jnp.where(number % 4 == 0, named(packed, number // 4), named(ordinary, number - number // 4 - 1))
    mixed = jax.random.permutation(jax.random.fold_in(own, 3), count)
    giver, sink = mixed[0:count // 2 * 2:2], mixed[1:count // 2 * 2:2]
    slack = jnp.minimum(sizes[giver] - 1, most - sizes[sink]) // 2
    slack = jnp.where((giver == ranking[0]) | (sink == ranking[0]) | (sizes[sink] == 0), 0, jnp.maximum(slack, 0))
    shifted = jax.random.randint(jax.random.fold_in(own, 4), (count // 2,), 0, 1 << 20) % (slack + 1)
    sizes = sizes.at[giver].add(-shifted).at[sink].add(shifted)
    labels = jnp.searchsorted(jnp.cumsum(sizes), jnp.arange(rows * top), side="right").astype(jnp.int32)
    table = labels.reshape(top, rows).T
    table = table[jax.random.permutation(jax.random.fold_in(own, 1), rows)]
    turn = jax.random.randint(jax.random.fold_in(own, 2), (rows, 1), 0, top)
    return jnp.take_along_axis(table, (jnp.arange(top)[None, :] + turn) % top, axis=1)


def portions_of(count, total, most, skew, full):
    loads = [(1 << 20) // math.isqrt(rank ** skew) + 1 for rank in range(1, count + 1)]
    largest = most if full else min(most, max(-(-total // count), total * loads[0] // sum(loads)))
    least = 1 if total - largest >= count - 1 else 0
    counts, rest = [largest] + [least] * (count - 1), total - largest - least * (count - 1)
    while rest > 0:
        free = [i for i in range(1, count) if counts[i] < largest] or [i for i in range(1, count) if counts[i] < most]
        pool, budget = sum([loads[i] for i in free]), rest
        for i in free:
            addition = min(most - counts[i], max(1, budget * loads[i] // pool), rest)
            counts[i] = counts[i] + addition
            rest = rest - addition
    return np.array(counts)


def gaussian(key, extent, width, most, cuts=(), kind=jnp.bfloat16):
    values = jax.random.normal(key, extent, jnp.float32) * width
    if len(cuts) > 0:
        values = levels(key, extent, cuts, -0.22, 0.18) * values
    return jnp.clip(values, min=-most, max=most).astype(kind)


def setup_inputs(seed: int = 0) -> dict:
    splits = jax.random.split(jax.random.key(seed), 19)
    hidden_in = gaussian(splits[0], (TOKENS, D), 0.5, 4.0, ((0, 8),))
    queries = draw_queries(jax.random.fold_in(splits[18], 71), 0)
    new_keys = gaussian(splits[2], (TOKENS, HEADS * HD), 2.5, 10.0, ((0, 8), (1, 4)))
    new_values = gaussian(splits[3], (TOKENS, HEADS * HD), 1.5, 8.0, ((0, 8), (1, 4)))
    key_cache = draw_key_cache(jax.random.fold_in(splits[18], 71), 0)
    value_cache = gaussian(splits[5], (TOKENS, MAXLEN, HEADS * HD), 1.0, 6.0, ((0, 8), (2, 4)))
    lengths = draw_lengths(jax.random.fold_in(splits[18], 71), 0)
    out_proj = gaussian(splits[7], (HEADS * HD, D), HD ** -0.5, 0.5, ((0, 4),))
    norm_gain = jnp.clip(1.0 + 0.18 * jax.random.normal(splits[8], (D,), jnp.float32), 0.1, 1.9)
    shared_gate = gaussian(splits[9], (SH, D), D ** -0.5, 0.125, ((0, 32),))
    shared_up = gaussian(splits[10], (SH, D), D ** -0.5, 0.125, ((0, 32),))
    shared_down = gaussian(splits[11], (SH, D), SH ** -0.5, 0.078125, ((0, 32),))
    shared_score = gaussian(splits[12], (D,), D ** -0.5, 0.125, (), jnp.float32)
    expert_gate = gaussian(splits[13], (EXPERTS, D, EFF), D ** -0.5, 0.125, ((0, 8), (2, 4)))
    expert_up = gaussian(splits[14], (EXPERTS, D, EFF), D ** -0.5, 0.125, ((0, 8), (2, 4)))
    expert_down = gaussian(splits[15], (EXPERTS, EFF, D), EFF ** -0.5, 0.15625, ((0, 8), (1, 4)))
    expert_ids_keys = jax.random.split(jax.random.fold_in(splits[16], 1), TOKENS // B_DEV)
    expert_ids_turns = jax.random.permutation(jax.random.fold_in(splits[16], 3), TOKENS // B_DEV)
    expert_ids = jax.vmap(lambda own, number: deal_out(jax.random.fold_in(splits[16], 2), own, number, B_DEV, EXPERTS, TOPK, CAP, 2))(expert_ids_keys, expert_ids_turns).reshape((TOKENS, TOPK))
    route_weight = jnp.clip(jnp.exp(math.log(0.59765625) - 1.7917595 * jax.random.uniform(splits[17], (TOKENS, TOPK), jnp.float32) ** levels(splits[17], (TOKENS, TOPK), ((0, 8),), -0.2, 0.2)), 0.099609375, 0.59765625).astype(jnp.bfloat16)
    return dict(hidden_in=hidden_in, queries=queries, new_keys=new_keys, new_values=new_values, key_cache=key_cache, value_cache=value_cache, lengths=lengths, out_proj=out_proj, norm_gain=norm_gain, shared_gate=shared_gate, shared_up=shared_up, shared_down=shared_down, shared_score=shared_score, expert_gate=expert_gate, expert_up=expert_up, expert_down=expert_down, expert_ids=expert_ids, route_weight=route_weight)


EPSILON = 1e-06

def attend(queries, new_keys, new_values, key_cache, value_cache, lengths):
    row_count = queries.shape[0]
    key_span = key_cache.shape[1]
    score_scale = HD ** (-0.5)
    query_heads = queries.reshape(row_count, HEADS, HD).astype(jnp.float32)
    own_keys = new_keys.reshape(row_count, HEADS, HD).astype(jnp.float32)
    own_values = new_values.reshape(row_count, HEADS, HD).astype(jnp.float32)
    cache_keys = key_cache.reshape(row_count, key_span, HEADS, HD).astype(jnp.float32)
    cache_values = value_cache.reshape(row_count, key_span, HEADS, HD).astype(jnp.float32)
    scores = jnp.einsum('bhd,blhd->bhl', query_heads, cache_keys) * score_scale
    own_score = jnp.einsum('bhd,bhd->bh', query_heads, own_keys) * score_scale
    live_keys = jnp.arange(key_span, dtype=jnp.int32)[None, None, :] < lengths[:, None, None]
    highest = jnp.maximum(lax.optimization_barrier(jnp.max(jnp.where(live_keys, scores, -1e+30), axis=-1)), own_score)
    weights = jnp.where(live_keys, jnp.exp(scores - highest[..., None]), 0.0)
    own_weight = jnp.exp(own_score - highest)
    totals = lax.optimization_barrier(jnp.sum(weights, axis=-1)) + own_weight
    probs = (weights / totals[..., None]).astype(jnp.bfloat16)
    own_prob = (own_weight / totals).astype(jnp.bfloat16)
    mixed = jnp.einsum('bhl,blhd->bhd', probs.astype(jnp.float32), cache_values)
    mixed = mixed + own_prob.astype(jnp.float32)[..., None] * own_values
    return mixed.astype(jnp.bfloat16).reshape(row_count, HEADS * HD)

def normalize(residual, norm_gain):
    values = residual.astype(jnp.float32)
    mean_square = lax.optimization_barrier(jnp.mean(values * values, axis=-1, keepdims=True))
    return (values * lax.rsqrt(mean_square + EPSILON) * norm_gain).astype(jnp.bfloat16)

def reference(hidden_in, queries, new_keys, new_values, key_cache, value_cache, lengths, out_proj, norm_gain, shared_gate, shared_up, shared_down, shared_score, expert_gate, expert_up, expert_down, expert_ids, route_weight):
    block_count = TOKENS // B_DEV
    pieces = (queries, new_keys, new_values, key_cache, value_cache, lengths)
    stacked = tuple((array.reshape((block_count, B_DEV) + array.shape[1:]) for array in pieces))

    def block_attend(block):
        return attend(*block)
    attended = lax.map(block_attend, stacked).reshape(TOKENS, HEADS * HD)
    attn_out = jnp.dot(attended, out_proj, preferred_element_type=jnp.float32)
    residual = (hidden_in.astype(jnp.float32) + attn_out).astype(jnp.bfloat16)
    normed = normalize(residual, norm_gain)
    normed_wide = normed.astype(jnp.float32)
    contract = (((1,), (1,)), ((), ()))
    shared_g = lax.dot_general(normed, shared_gate, contract, preferred_element_type=jnp.float32)
    shared_u = lax.dot_general(normed, shared_up, contract, preferred_element_type=jnp.float32)
    shared_hidden = (jax.nn.silu(shared_g) * shared_u).astype(jnp.bfloat16)
    shared_sum = jnp.dot(shared_hidden, shared_down, preferred_element_type=jnp.float32)
    gate_scale = jax.nn.sigmoid(jnp.dot(normed_wide, shared_score, precision=lax.Precision.HIGHEST))

    def one_expert(total, block):
        gate_w, up_w, down_w, index = block
        gate = jnp.dot(normed_wide, gate_w.astype(jnp.float32), precision=lax.Precision.HIGHEST)
        up_proj = jnp.dot(normed_wide, up_w.astype(jnp.float32), precision=lax.Precision.HIGHEST)
        inner = (jax.nn.silu(gate) * up_proj).astype(jnp.bfloat16)
        result = jnp.dot(inner.astype(jnp.float32), down_w.astype(jnp.float32), precision=lax.Precision.HIGHEST)
        weight = lax.optimization_barrier(jnp.sum(jnp.where(expert_ids == index, route_weight.astype(jnp.float32), 0.0), axis=1))
        return (total + weight[:, None] * result, None)
    start_total = jnp.zeros((TOKENS, D), jnp.float32)
    routed, _ = lax.scan(one_expert, start_total, (expert_gate, expert_up, expert_down, jnp.arange(EXPERTS, dtype=jnp.int32)))
    layer_out = residual.astype(jnp.float32) + gate_scale[:, None] * shared_sum + routed
    return layer_out.astype(jnp.bfloat16)
```

```python
import functools

import jax
import jax.numpy as jnp
from jax import lax
from jax.experimental import pallas as pl
from jax.experimental.pallas import tpu as pltpu
from jax.sharding import PartitionSpec as P

HD = 128
EPSILON = 1e-06
CHUNK = 256
MESH = pl.DeviceIdType.MESH


def attend_kernel(
    lengths_ref, q_ref, nk_ref, nv_ref, k_hbm, v_hbm, proj_hbm, out_ref,
    k_buf, v_buf, proj_buf, attended, k_sem, v_sem, proj_sem,
):
    rows, span, width = k_buf.shape
    heads = width // HD
    chunks = span // CHUNK
    scale = HD ** (-0.5)

    def k_copy(b, c):
        part = pl.ds(c * CHUNK, CHUNK)
        return pltpu.make_async_copy(k_hbm.at[b, part], k_buf.at[b, part], k_sem.at[b, c])

    def v_copy(b, c):
        part = pl.ds(c * CHUNK, CHUNK)
        return pltpu.make_async_copy(v_hbm.at[b, part], v_buf.at[b, part], v_sem.at[b, c])

    def live(b, c):
        return lengths_ref[b] > c * CHUNK

    for copy in (k_copy, v_copy):
        for b in range(rows):
            for c in range(chunks):
                @pl.when(live(b, c))
                def _():
                    copy(b, c).start()
    proj_copy = pltpu.make_async_copy(proj_hbm, proj_buf, proj_sem)
    proj_copy.start()
    for b in range(rows):
        for c in range(1, chunks):
            @pl.when(jnp.logical_not(live(b, c)))
            def _():
                v_buf[b, c * CHUNK:(c + 1) * CHUNK, :] = jnp.zeros((CHUNK, width), v_buf.dtype)
    for b in range(rows):
        for c in range(chunks):
            @pl.when(live(b, c))
            def _():
                k_copy(b, c).wait()

    group = max(8, heads)
    row_id = lax.broadcasted_iota(jnp.int32, (group, width), 0)
    lane_head = lax.broadcasted_iota(jnp.int32, (group, width), 1) // HD
    own_head = row_id == lane_head
    position = lax.broadcasted_iota(jnp.int32, (group, span), 1)
    queries = q_ref[...].astype(jnp.float32)
    own_keys = nk_ref[...].astype(jnp.float32)
    own_values = nv_ref[...].astype(jnp.float32)
    probs = []
    own_probs = []
    for b in range(rows):
        spread = jnp.where(own_head, queries[b:b + 1, :], 0.0)
        scores = lax.dot_general(
            spread.astype(jnp.bfloat16), k_buf[b], (((1,), (1,)), ((), ())),
            preferred_element_type=jnp.float32,
        ) * scale
        own_score = jnp.sum(spread * own_keys[b:b + 1, :], axis=1, keepdims=True) * scale
        alive = position < lengths_ref[b]
        scores = jnp.where(alive, scores, -1e30)
        highest = jnp.maximum(jnp.max(scores, axis=1, keepdims=True), own_score)
        weights = jnp.where(alive, jnp.exp(scores - highest), 0.0)
        own_weight = jnp.exp(own_score - highest)
        total = jnp.sum(weights, axis=1, keepdims=True) + own_weight
        probs.append((weights / total).astype(jnp.bfloat16))
        own_probs.append((own_weight / total).astype(jnp.bfloat16).astype(jnp.float32))
    for b in range(rows):
        for c in range(chunks):
            @pl.when(live(b, c))
            def _():
                v_copy(b, c).wait()
    for b in range(rows):
        mixed = jnp.dot(probs[b], v_buf[b], preferred_element_type=jnp.float32)
        mixed = mixed + own_probs[b] * own_values[b:b + 1, :]
        attended[b:b + 1, :] = jnp.sum(jnp.where(own_head, mixed, 0.0), axis=0, keepdims=True)
    proj_copy.wait()
    out_ref[...] = jnp.dot(
        attended[...].astype(jnp.bfloat16), proj_buf[...], preferred_element_type=jnp.float32
    )


def silu(x):
    return x / (1.0 + jnp.exp(-x))


def expert_kernel(
    req_count, head_count,
    part_ref, hid_ref, gain_ref, score_ref, ids_ref, rw_ref,
    sg_hbm, su_hbm, sd_hbm, eg_hbm, eu_hbm, ed_hbm,
    out_ref,
    sg, su, sd, eg, eu, ed, weight_sems,
    w_all, terms1, resid_all, send5, terms5, total6, send6, terms6, final,
    w_send, w_recv, s1, r1, s2, r2, s3, r3, s5, r5, s6, r6, s7, r7,
):
    rows, model = hid_ref.shape
    cols = model // head_count
    tokens = req_count * rows
    me_r = lax.axis_index("req")
    me_h = lax.axis_index("head")

    loads = [
        pltpu.make_async_copy(src, dst, weight_sems.at[i])
        for i, (src, dst) in enumerate((
            (eg_hbm.at[0], eg), (eu_hbm.at[0], eu), (sg_hbm, sg), (su_hbm, su),
            (sd_hbm, sd), (ed_hbm.at[0], ed),
        ))
    ]
    for load in loads:
        load.start()

    def req_peer(d):
        return lax.rem(me_r + d, req_count)

    def req_source(d):
        return lax.rem(me_r + (req_count - d), req_count)

    def head_peer(d):
        return lax.rem(me_h + d, head_count)

    def head_source(d):
        return lax.rem(me_h + (head_count - d), head_count)

    def remote(src, dst, send, recv, r, h):
        return pltpu.make_async_remote_copy(
            src_ref=src, dst_ref=dst, send_sem=send, recv_sem=recv,
            device_id=(r, h), device_id_type=MESH,
        )

    barrier = pltpu.get_barrier_semaphore()
    for d in range(1, head_count):
        pl.semaphore_signal(barrier, inc=1, device_id=(me_r, head_peer(d)), device_id_type=MESH)
    for d in range(1, req_count):
        pl.semaphore_signal(barrier, inc=1, device_id=(req_peer(d), me_h), device_id_type=MESH)
    lane = lax.broadcasted_iota(jnp.int32, (rows, 128), 1)
    table = jnp.zeros((rows, 128), jnp.float32)
    route = rw_ref[...].astype(jnp.float32)
    ids = ids_ref[...]
    for k in range(ids.shape[1]):
        table = table + jnp.where(ids[:, k:k + 1] == lane, route[:, k:k + 1], 0.0)
    w_all[me_r] = table
    pl.semaphore_wait(barrier, head_count + req_count - 2)

    def my_cols(h):
        return pl.ds(pl.multiple_of(h * cols, 128), cols)

    sends = []

    def start(copy):
        copy.start()
        sends.append(copy)

    for d in range(1, head_count):
        start(remote(
            part_ref.at[:, my_cols(head_peer(d))], terms1.at[d], s1.at[d], r1.at[d],
            me_r, head_peer(d),
        ))
    for d in range(1, req_count):
        start(remote(
            w_all.at[me_r], w_all.at[me_r], w_send.at[d], w_recv.at[d], req_peer(d), me_h,
        ))
    summed = part_ref[:, my_cols(me_h)]
    for d in range(1, head_count):
        remote(
            part_ref.at[:, my_cols(me_h)], terms1.at[d], s1.at[d], r1.at[d], me_r, head_peer(d),
        ).wait_recv()
        summed = summed + terms1[d]
    resid = (hid_ref[:, my_cols(me_h)].astype(jnp.float32) + summed).astype(jnp.bfloat16)
    resid_all[me_h, me_r] = resid

    for d in range(1, req_count):
        block = resid_all.at[me_h, me_r]
        start(remote(block, block, s2.at[d], r2.at[d], req_peer(d), me_h))
    for j in range(req_count):
        block = resid_all.at[me_h, req_source(j)]
        if j > 0:
            remote(block, block, s2.at[j], r2.at[j], req_peer(j), me_h).wait_recv()
        for d in range(1, head_count):
            start(remote(block, block, s3.at[d, j], r3.at[d, j], me_r, head_peer(d)))
    for j in range(req_count):
        for d in range(1, head_count):
            block = resid_all.at[head_source(d), req_source(j)]
            remote(block, block, s3.at[d, j], r3.at[d, j], me_r, head_peer(d)).wait_recv()

    wide = [
        resid_all[h].astype(jnp.float32).reshape(tokens, cols) for h in range(head_count)
    ]
    square = jnp.sum(wide[0] * wide[0], axis=1, keepdims=True)
    for h in range(1, head_count):
        square = square + jnp.sum(wide[h] * wide[h], axis=1, keepdims=True)
    inverse = lax.rsqrt(square / model + EPSILON)
    normed = [
        (wide[h] * inverse * gain_ref[:, h * cols:(h + 1) * cols]).astype(jnp.bfloat16)
        for h in range(head_count)
    ]
    logit = jnp.zeros((tokens, 1), jnp.float32)
    for h in range(head_count):
        logit = logit + jnp.sum(
            normed[h].astype(jnp.float32) * score_ref[:, h * cols:(h + 1) * cols],
            axis=1, keepdims=True,
        )
    gate_scale = 1.0 / (1.0 + jnp.exp(-logit))
    for load in loads:
        load.wait()

    def project(weight):
        out = None
        for h in range(head_count):
            term = jnp.dot(
                normed[h], weight[h * cols:(h + 1) * cols, :], preferred_element_type=jnp.float32
            )
            out = term if out is None else out + term
        return out

    def project_t(weight):
        out = None
        for h in range(head_count):
            term = lax.dot_general(
                normed[h], weight[:, h * cols:(h + 1) * cols], (((1,), (1,)), ((), ())),
                preferred_element_type=jnp.float32,
            )
            out = term if out is None else out + term
        return out

    inner = (silu(project(eg)) * project(eu)).astype(jnp.bfloat16)
    shared = (silu(project_t(sg)) * project_t(su)).astype(jnp.bfloat16)
    for d in range(1, req_count):
        block = w_all.at[req_source(d)]
        remote(block, block, w_send.at[d], w_recv.at[d], req_peer(d), me_h).wait_recv()
    weights = w_all[...].reshape(tokens, 128)
    wide_lane = lax.broadcasted_iota(jnp.int32, (tokens, 128), 1)
    weight = jnp.sum(jnp.where(wide_lane == me_r, weights, 0.0), axis=1, keepdims=True)

    def column_terms(h):
        part = my_cols(h)
        term = gate_scale * jnp.dot(shared, sd[:, part], preferred_element_type=jnp.float32)
        term = term + weight * jnp.dot(inner, ed[:, part], preferred_element_type=jnp.float32)
        return term.reshape(req_count, rows, cols)

    for d in range(1, head_count):
        send5[d] = column_terms(head_peer(d)).astype(jnp.bfloat16)
        start(remote(send5.at[d], terms5.at[d], s5.at[d], r5.at[d], me_r, head_peer(d)))
    total = column_terms(me_h)
    for d in range(1, head_count):
        remote(
            send5.at[d], terms5.at[d], s5.at[d], r5.at[d], me_r, head_peer(d)
        ).wait_recv()
        total = total + terms5[d].astype(jnp.float32)
    total6[...] = total
    send6[...] = total.astype(jnp.bfloat16)
    for d in range(1, req_count):
        start(remote(
            send6.at[req_peer(d)], terms6.at[d], s6.at[d], r6.at[d], req_peer(d), me_h
        ))
    combined = total6[me_r]
    for d in range(1, req_count):
        remote(
            send6.at[req_peer(d)], terms6.at[d], s6.at[d], r6.at[d], req_peer(d), me_h
        ).wait_recv()
        combined = combined + terms6[d].astype(jnp.float32)
    final[me_h] = (resid.astype(jnp.float32) + combined).astype(jnp.bfloat16)
    for d in range(1, head_count):
        start(remote(
            final.at[me_h], final.at[me_h], s7.at[d], r7.at[d], me_r, head_peer(d)
        ))
    for d in range(1, head_count):
        block = final.at[head_source(d)]
        remote(block, block, s7.at[d], r7.at[d], me_r, head_peer(d)).wait_recv()
    for h in range(head_count):
        out_ref[:, h * cols:(h + 1) * cols] = final[h]
    for copy in sends:
        copy.wait_send()


VMEM_SPEC = pl.BlockSpec(memory_space=pltpu.VMEM)
ANY_SPEC = pl.BlockSpec(memory_space=pl.ANY)


def per_device(
    req_count, head_count,
    hidden_in, queries, new_keys, new_values, key_cache, value_cache, lengths, out_proj,
    norm_gain, shared_gate, shared_up, shared_down, shared_score, expert_gate, expert_up,
    expert_down, expert_ids, route_weight,
):
    rows, model = hidden_in.shape
    span, width = key_cache.shape[1:]
    bf16, f32 = jnp.bfloat16, jnp.float32
    dma = pltpu.SemaphoreType.DMA
    chunks = span // CHUNK
    partial = pl.pallas_call(
        attend_kernel,
        out_shape=jax.ShapeDtypeStruct((rows, model), f32),
        in_specs=[pl.BlockSpec(memory_space=pltpu.SMEM)] + [VMEM_SPEC] * 3 + [ANY_SPEC] * 3,
        out_specs=VMEM_SPEC,
        scratch_shapes=[
            pltpu.VMEM((rows, span, width), bf16),
            pltpu.VMEM((rows, span, width), bf16),
            pltpu.VMEM(out_proj.shape, bf16),
            pltpu.VMEM((rows, width), f32),
            dma((rows, chunks)), dma((rows, chunks)), dma,
        ],
        compiler_params=pltpu.CompilerParams(vmem_limit_bytes=40 << 20),
        name="attend",
    )(lengths, queries, new_keys, new_values, key_cache, value_cache, out_proj)

    cols = model // head_count
    return pl.pallas_call(
        functools.partial(expert_kernel, req_count, head_count),
        out_shape=jax.ShapeDtypeStruct((rows, model), bf16),
        in_specs=[VMEM_SPEC] * 6 + [ANY_SPEC] * 6,
        out_specs=VMEM_SPEC,
        scratch_shapes=[
            pltpu.VMEM(shared_gate.shape, bf16),
            pltpu.VMEM(shared_up.shape, bf16),
            pltpu.VMEM(shared_down.shape, bf16),
            pltpu.VMEM(expert_gate.shape[1:], bf16),
            pltpu.VMEM(expert_up.shape[1:], bf16),
            pltpu.VMEM(expert_down.shape[1:], bf16),
            dma((6,)),
            pltpu.VMEM((req_count, rows, 128), f32),
            pltpu.VMEM((head_count, rows, cols), f32),
            pltpu.VMEM((head_count, req_count, rows, cols), bf16),
            pltpu.VMEM((head_count, req_count, rows, cols), bf16),
            pltpu.VMEM((head_count, req_count, rows, cols), bf16),
            pltpu.VMEM((req_count, rows, cols), f32),
            pltpu.VMEM((req_count, rows, cols), bf16),
            pltpu.VMEM((req_count, rows, cols), bf16),
            pltpu.VMEM((head_count, rows, cols), bf16),
            dma((req_count,)), dma((req_count,)),
            dma((head_count,)), dma((head_count,)),
            dma((req_count,)), dma((req_count,)),
            dma((head_count, req_count)), dma((head_count, req_count)),
            dma((head_count,)), dma((head_count,)),
            dma((req_count,)), dma((req_count,)),
            dma((head_count,)), dma((head_count,)),
        ],
        compiler_params=pltpu.CompilerParams(
            vmem_limit_bytes=40 << 20, collective_id=0, has_side_effects=True
        ),
        name="experts",
    )(
        partial, hidden_in, norm_gain.reshape(1, model), shared_score.reshape(1, model),
        expert_ids, route_weight,
        shared_gate, shared_up, shared_down, expert_gate, expert_up, expert_down,
    )


def solution(mesh):
    in_specs = (
        P("req", None),
        P("req", "head"),
        P("req", "head"),
        P("req", "head"),
        P("req", None, "head"),
        P("req", None, "head"),
        P("req"),
        P("head", None),
        P(),
        P(("req", "head"), None),
        P(("req", "head"), None),
        P(("req", "head"), None),
        P(),
        P("req", None, "head"),
        P("req", None, "head"),
        P("req", "head", None),
        P("req", None),
        P("req", None),
    )
    body = functools.partial(per_device, mesh.shape["req"], mesh.shape["head"])
    return jax.shard_map(
        body, mesh=mesh, in_specs=in_specs, out_specs=P("req", None), check_vma=False
    )
```

```python
import functools

import jax
import jax.numpy as jnp
from jax import lax
from jax.experimental import pallas as pl
from jax.experimental.pallas import tpu as pltpu
from jax.sharding import PartitionSpec as P

HD = 128
EPSILON = 1e-06
CHUNK = 256
MESH = pl.DeviceIdType.MESH


def attend_kernel(
    lengths_hbm, q_hbm, nk_hbm, nv_hbm, k_hbm, v_hbm, proj_hbm, out_ref,
    lengths_ref, q_ref, nk_ref, nv_ref,
    k_buf, v_buf, proj_buf, attended, k_sem, v_sem, proj_sem, small_sem,
):
    small = [
        pltpu.make_async_copy(src, dst, small_sem.at[i])
        for i, (src, dst) in enumerate((
            (lengths_hbm, lengths_ref), (q_hbm, q_ref), (nk_hbm, nk_ref), (nv_hbm, nv_ref),
        ))
    ]
    for copy in small:
        copy.start()
    small[0].wait()
    rows, span, width = k_buf.shape
    heads = width // HD
    chunks = span // CHUNK
    scale = HD ** (-0.5)

    def k_copy(b, c):
        part = pl.ds(c * CHUNK, CHUNK)
        return pltpu.make_async_copy(k_hbm.at[b, part], k_buf.at[b, part], k_sem.at[b, c])

    def v_copy(b, c):
        part = pl.ds(c * CHUNK, CHUNK)
        return pltpu.make_async_copy(v_hbm.at[b, part], v_buf.at[b, part], v_sem.at[b, c])

    def live(b, c):
        return lengths_ref[b] > c * CHUNK

    for copy in (k_copy, v_copy):
        for b in range(rows):
            for c in range(chunks):
                @pl.when(live(b, c))
                def _():
                    copy(b, c).start()
    proj_copy = pltpu.make_async_copy(proj_hbm, proj_buf, proj_sem)
    proj_copy.start()
    for b in range(rows):
        for c in range(1, chunks):
            @pl.when(jnp.logical_not(live(b, c)))
            def _():
                v_buf[b, c * CHUNK:(c + 1) * CHUNK, :] = jnp.zeros((CHUNK, width), v_buf.dtype)
    for b in range(rows):
        for c in range(chunks):
            @pl.when(live(b, c))
            def _():
                k_copy(b, c).wait()

    for copy in small[1:]:
        copy.wait()
    group = max(8, heads)
    row_id = lax.broadcasted_iota(jnp.int32, (group, width), 0)
    lane_head = lax.broadcasted_iota(jnp.int32, (group, width), 1) // HD
    own_head = row_id == lane_head
    position = lax.broadcasted_iota(jnp.int32, (group, span), 1)
    queries = q_ref[...].astype(jnp.float32)
    own_keys = nk_ref[...].astype(jnp.float32)
    own_values = nv_ref[...].astype(jnp.float32)
    probs = []
    own_probs = []
    for b in range(rows):
        spread = jnp.where(own_head, queries[b:b + 1, :], 0.0)
        scores = lax.dot_general(
            spread.astype(jnp.bfloat16), k_buf[b], (((1,), (1,)), ((), ())),
            preferred_element_type=jnp.float32,
        ) * scale
        own_score = jnp.sum(spread * own_keys[b:b + 1, :], axis=1, keepdims=True) * scale
        alive = position < lengths_ref[b]
        scores = jnp.where(alive, scores, -1e30)
        highest = jnp.maximum(jnp.max(scores, axis=1, keepdims=True), own_score)
        weights = jnp.where(alive, jnp.exp(scores - highest), 0.0)
        own_weight = jnp.exp(own_score - highest)
        total = jnp.sum(weights, axis=1, keepdims=True) + own_weight
        probs.append((weights / total).astype(jnp.bfloat16))
        own_probs.append((own_weight / total).astype(jnp.bfloat16).astype(jnp.float32))
    for b in range(rows):
        for c in range(chunks):
            @pl.when(live(b, c))
            def _():
                v_copy(b, c).wait()
    for b in range(rows):
        mixed = jnp.dot(probs[b], v_buf[b], preferred_element_type=jnp.float32)
        mixed = mixed + own_probs[b] * own_values[b:b + 1, :]
        attended[b:b + 1, :] = jnp.sum(jnp.where(own_head, mixed, 0.0), axis=0, keepdims=True)
    proj_copy.wait()
    out_ref[...] = jnp.dot(
        attended[...].astype(jnp.bfloat16), proj_buf[...], preferred_element_type=jnp.float32
    )


def silu(x):
    return x / (1.0 + jnp.exp(-x))


def expert_kernel(
    req_count, head_count,
    part_ref, hid_hbm, gain_hbm, score_hbm, ids_hbm, rw_hbm,
    sg_hbm, su_hbm, sd_hbm, eg_hbm, eu_hbm, ed_hbm,
    out_ref,
    hid_ref, gain_ref, score_ref, ids_ref, rw_ref, small_sems,
    sg, su, sd, eg, eu, ed, weight_sems,
    w_all, terms1, resid_all, send5, terms5, total6, send6, terms6, final,
    w_send, w_recv, s1, r1, s2, r2, s3, r3, s5, r5, s6, r6, s7, r7,
):
    rows, model = hid_ref.shape
    cols = model // head_count
    tokens = req_count * rows
    me_r = lax.axis_index("req")
    me_h = lax.axis_index("head")

    small = [
        pltpu.make_async_copy(src, dst, small_sems.at[i])
        for i, (src, dst) in enumerate((
            (ids_hbm, ids_ref), (rw_hbm, rw_ref), (hid_hbm, hid_ref), (gain_hbm, gain_ref),
            (score_hbm, score_ref),
        ))
    ]
    for load in small:
        load.start()
    loads = [
        pltpu.make_async_copy(src, dst, weight_sems.at[i])
        for i, (src, dst) in enumerate((
            (eg_hbm.at[0], eg), (eu_hbm.at[0], eu), (sg_hbm, sg), (su_hbm, su),
            (sd_hbm, sd), (ed_hbm.at[0], ed),
        ))
    ]
    for load in loads:
        load.start()

    def req_peer(d):
        return lax.rem(me_r + d, req_count)

    def req_source(d):
        return lax.rem(me_r + (req_count - d), req_count)

    def head_peer(d):
        return lax.rem(me_h + d, head_count)

    def head_source(d):
        return lax.rem(me_h + (head_count - d), head_count)

    def remote(src, dst, send, recv, r, h):
        return pltpu.make_async_remote_copy(
            src_ref=src, dst_ref=dst, send_sem=send, recv_sem=recv,
            device_id=(r, h), device_id_type=MESH,
        )

    barrier = pltpu.get_barrier_semaphore()
    for d in range(1, head_count):
        pl.semaphore_signal(barrier, inc=1, device_id=(me_r, head_peer(d)), device_id_type=MESH)
    for d in range(1, req_count):
        pl.semaphore_signal(barrier, inc=1, device_id=(req_peer(d), me_h), device_id_type=MESH)
    lane = lax.broadcasted_iota(jnp.int32, (rows, 128), 1)
    table = jnp.zeros((rows, 128), jnp.float32)
    for load in small:
        load.wait()
    route = rw_ref[...].astype(jnp.float32)
    ids = ids_ref[...].astype(jnp.float32)
    diagonal = (
        lax.broadcasted_iota(jnp.int32, (rows, rows), 0)
        == lax.broadcasted_iota(jnp.int32, (rows, rows), 1)
    )
    lane_value = lane.astype(jnp.float32)
    for k in range(ids.shape[0]):
        chosen = jnp.sum(jnp.where(diagonal, ids[k:k + 1, :], 0.0), axis=1, keepdims=True)
        share = jnp.sum(jnp.where(diagonal, route[k:k + 1, :], 0.0), axis=1, keepdims=True)
        table = table + jnp.where(chosen == lane_value, share, 0.0)
    w_all[me_r] = table
    pl.semaphore_wait(barrier, head_count + req_count - 2)

    def my_cols(h):
        return pl.ds(pl.multiple_of(h * cols, 128), cols)

    sends = []

    def start(copy):
        copy.start()
        sends.append(copy)

    for d in range(1, head_count):
        start(remote(
            part_ref.at[:, my_cols(head_peer(d))], terms1.at[d], s1.at[d], r1.at[d],
            me_r, head_peer(d),
        ))
    for d in range(1, req_count):
        start(remote(
            w_all.at[me_r], w_all.at[me_r], w_send.at[d], w_recv.at[d], req_peer(d), me_h,
        ))
    summed = part_ref[:, my_cols(me_h)]
    for d in range(1, head_count):
        remote(
            part_ref.at[:, my_cols(me_h)], terms1.at[d], s1.at[d], r1.at[d], me_r, head_peer(d),
        ).wait_recv()
        summed = summed + terms1[d]
    resid = (hid_ref[:, my_cols(me_h)].astype(jnp.float32) + summed).astype(jnp.bfloat16)
    resid_all[me_h, me_r] = resid

    for d in range(1, req_count):
        block = resid_all.at[me_h, me_r]
        start(remote(block, block, s2.at[d], r2.at[d], req_peer(d), me_h))
    for j in range(req_count):
        block = resid_all.at[me_h, req_source(j)]
        if j > 0:
            remote(block, block, s2.at[j], r2.at[j], req_peer(j), me_h).wait_recv()
        for d in range(1, head_count):
            start(remote(block, block, s3.at[d, j], r3.at[d, j], me_r, head_peer(d)))
    for j in range(req_count):
        for d in range(1, head_count):
            block = resid_all.at[head_source(d), req_source(j)]
            remote(block, block, s3.at[d, j], r3.at[d, j], me_r, head_peer(d)).wait_recv()

    wide = [
        resid_all[h].astype(jnp.float32).reshape(tokens, cols) for h in range(head_count)
    ]
    square = jnp.sum(wide[0] * wide[0], axis=1, keepdims=True)
    for h in range(1, head_count):
        square = square + jnp.sum(wide[h] * wide[h], axis=1, keepdims=True)
    inverse = lax.rsqrt(square / model + EPSILON)
    normed = [
        (wide[h] * inverse * gain_ref[:, h * cols:(h + 1) * cols]).astype(jnp.bfloat16)
        for h in range(head_count)
    ]
    logit = jnp.zeros((tokens, 1), jnp.float32)
    for h in range(head_count):
        logit = logit + jnp.sum(
            normed[h].astype(jnp.float32) * score_ref[:, h * cols:(h + 1) * cols],
            axis=1, keepdims=True,
        )
    gate_scale = 1.0 / (1.0 + jnp.exp(-logit))
    for load in loads:
        load.wait()

    def project_t(weight):
        out = None
        for h in range(head_count):
            term = lax.dot_general(
                normed[h], weight[:, h * cols:(h + 1) * cols], (((1,), (1,)), ((), ())),
                preferred_element_type=jnp.float32,
            )
            out = term if out is None else out + term
        return out

    inner = (silu(project_t(eg)) * project_t(eu)).astype(jnp.bfloat16)
    shared = (silu(project_t(sg)) * project_t(su)).astype(jnp.bfloat16)
    for d in range(1, req_count):
        block = w_all.at[req_source(d)]
        remote(block, block, w_send.at[d], w_recv.at[d], req_peer(d), me_h).wait_recv()
    weights = w_all[...].reshape(tokens, 128)
    wide_lane = lax.broadcasted_iota(jnp.int32, (tokens, 128), 1)
    weight = jnp.sum(jnp.where(wide_lane == me_r, weights, 0.0), axis=1, keepdims=True)

    def column_terms(h):
        part = my_cols(h)
        term = gate_scale * jnp.dot(shared, sd[:, part], preferred_element_type=jnp.float32)
        term = term + weight * jnp.dot(inner, ed[:, part], preferred_element_type=jnp.float32)
        return term.reshape(req_count, rows, cols)

    for d in range(1, head_count):
        send5[d] = column_terms(head_peer(d)).astype(jnp.bfloat16)
        start(remote(send5.at[d], terms5.at[d], s5.at[d], r5.at[d], me_r, head_peer(d)))
    total = column_terms(me_h)
    for d in range(1, head_count):
        remote(
            send5.at[d], terms5.at[d], s5.at[d], r5.at[d], me_r, head_peer(d)
        ).wait_recv()
        total = total + terms5[d].astype(jnp.float32)
    total6[...] = total
    send6[...] = total.astype(jnp.bfloat16)
    for d in range(1, req_count):
        start(remote(
            send6.at[req_peer(d)], terms6.at[d], s6.at[d], r6.at[d], req_peer(d), me_h
        ))
    combined = total6[me_r]
    for d in range(1, req_count):
        remote(
            send6.at[req_peer(d)], terms6.at[d], s6.at[d], r6.at[d], req_peer(d), me_h
        ).wait_recv()
        combined = combined + terms6[d].astype(jnp.float32)
    final[me_h] = (resid.astype(jnp.float32) + combined).astype(jnp.bfloat16)
    for d in range(1, head_count):
        start(remote(
            final.at[me_h], final.at[me_h], s7.at[d], r7.at[d], me_r, head_peer(d)
        ))
    for d in range(1, head_count):
        block = final.at[head_source(d)]
        remote(block, block, s7.at[d], r7.at[d], me_r, head_peer(d)).wait_recv()
    for h in range(head_count):
        out_ref[:, h * cols:(h + 1) * cols] = final[h]
    for copy in sends:
        copy.wait_send()


VMEM_SPEC = pl.BlockSpec(memory_space=pltpu.VMEM)
HBM_SPEC = pl.BlockSpec(memory_space=pltpu.HBM)


def per_device(
    req_count, head_count,
    hidden_in, queries, new_keys, new_values, key_cache, value_cache, lengths, out_proj,
    norm_gain, shared_gate, shared_up, shared_down, shared_score, expert_gate, expert_up,
    expert_down, expert_ids, route_weight,
):
    rows, model = hidden_in.shape
    span, width = key_cache.shape[1:]
    bf16, f32 = jnp.bfloat16, jnp.float32
    dma = pltpu.SemaphoreType.DMA
    chunks = span // CHUNK
    partial = pl.pallas_call(
        attend_kernel,
        out_shape=jax.ShapeDtypeStruct((rows, model), f32),
        in_specs=[HBM_SPEC] * 7,
        out_specs=VMEM_SPEC,
        scratch_shapes=[
            pltpu.SMEM((rows,), jnp.int32),
            pltpu.VMEM((rows, width), bf16),
            pltpu.VMEM((rows, width), bf16),
            pltpu.VMEM((rows, width), bf16),
            pltpu.VMEM((rows, span, width), bf16),
            pltpu.VMEM((rows, span, width), bf16),
            pltpu.VMEM(out_proj.shape, bf16),
            pltpu.VMEM((rows, width), f32),
            dma((rows, chunks)), dma((rows, chunks)), dma, dma((4,)),
        ],
        compiler_params=pltpu.CompilerParams(vmem_limit_bytes=64 << 20),
        name="attend",
    )(lengths, queries, new_keys, new_values, key_cache, value_cache, out_proj)

    cols = model // head_count
    return pl.pallas_call(
        functools.partial(expert_kernel, req_count, head_count),
        out_shape=jax.ShapeDtypeStruct((rows, model), bf16),
        in_specs=[VMEM_SPEC] + [HBM_SPEC] * 11,
        out_specs=VMEM_SPEC,
        scratch_shapes=[
            pltpu.VMEM((rows, model), bf16),
            pltpu.VMEM((1, model), f32),
            pltpu.VMEM((1, model), f32),
            pltpu.VMEM(expert_ids.shape[::-1], jnp.int32),
            pltpu.VMEM(route_weight.shape[::-1], bf16),
            dma((5,)),
            pltpu.VMEM(shared_gate.shape, bf16),
            pltpu.VMEM(shared_up.shape, bf16),
            pltpu.VMEM(shared_down.shape, bf16),
            pltpu.VMEM(expert_gate.shape[:0:-1], bf16),
            pltpu.VMEM(expert_up.shape[:0:-1], bf16),
            pltpu.VMEM(expert_down.shape[1:], bf16),
            dma((6,)),
            pltpu.VMEM((req_count, rows, 128), f32),
            pltpu.VMEM((head_count, rows, cols), f32),
            pltpu.VMEM((head_count, req_count, rows, cols), bf16),
            pltpu.VMEM((head_count, req_count, rows, cols), bf16),
            pltpu.VMEM((head_count, req_count, rows, cols), bf16),
            pltpu.VMEM((req_count, rows, cols), f32),
            pltpu.VMEM((req_count, rows, cols), bf16),
            pltpu.VMEM((req_count, rows, cols), bf16),
            pltpu.VMEM((head_count, rows, cols), bf16),
            dma((req_count,)), dma((req_count,)),
            dma((head_count,)), dma((head_count,)),
            dma((req_count,)), dma((req_count,)),
            dma((head_count, req_count)), dma((head_count, req_count)),
            dma((head_count,)), dma((head_count,)),
            dma((req_count,)), dma((req_count,)),
            dma((head_count,)), dma((head_count,)),
        ],
        compiler_params=pltpu.CompilerParams(
            vmem_limit_bytes=64 << 20, collective_id=0, has_side_effects=True
        ),
        name="experts",
    )(
        partial, hidden_in, norm_gain.reshape(1, model), shared_score.reshape(1, model),
        expert_ids.T, route_weight.T,
        shared_gate, shared_up, shared_down,
        jnp.swapaxes(expert_gate, 1, 2), jnp.swapaxes(expert_up, 1, 2), expert_down,
    )


def solution(mesh):
    in_specs = (
        P("req", None),
        P("req", "head"),
        P("req", "head"),
        P("req", "head"),
        P("req", None, "head"),
        P("req", None, "head"),
        P("req"),
        P("head", None),
        P(),
        P(("req", "head"), None),
        P(("req", "head"), None),
        P(("req", "head"), None),
        P(),
        P("req", None, "head"),
        P("req", None, "head"),
        P("req", "head", None),
        P("req", None),
        P("req", None),
    )
    body = functools.partial(per_device, mesh.shape["req"], mesh.shape["head"])
    return jax.shard_map(
        body, mesh=mesh, in_specs=in_specs, out_specs=P("req", None), check_vma=False
    )
```

```python
import functools

import jax
import jax.numpy as jnp
from jax import lax
from jax.experimental import pallas as pl
from jax.experimental.pallas import tpu as pltpu
from jax.sharding import PartitionSpec as P

HD = 128
EPSILON = 1e-06
MESH = pl.DeviceIdType.MESH


def silu(x):
    return x / (1.0 + jnp.exp(-x))


def layer_kernel(
    req_count, head_count,
    lengths_hbm, q_hbm, nk_hbm, nv_hbm, k_hbm, v_hbm, proj_hbm,
    hid_hbm, gain_hbm, score_hbm, ids_hbm, rw_hbm,
    sg_hbm, su_hbm, sd_hbm, eg_hbm, eu_hbm, ed_hbm,
    out_ref,
    lengths_ref, q_ref, nk_ref, nv_ref, k_buf, v_buf, proj_buf, k_sem, v_sem, proj_sem,
    attended, part_ref,
    hid_ref, gain_ref, score_ref, ids_ref, rw_ref, small_sems,
    sg, su, sd, eg, eu, ed, weight_sems,
    w_all, terms1, resid_all, send5, terms5, total6, send6, terms6, final,
    w_send, w_recv, s1, r1, s2, r2, s3, r3, s5, r5, s6, r6, s7, r7,
):
    rows, model = hid_ref.shape
    cols = model // head_count
    tokens = req_count * rows
    me_r = lax.axis_index("req")
    me_h = lax.axis_index("head")

    def req_peer(d):
        return lax.rem(me_r + d, req_count)

    def req_source(d):
        return lax.rem(me_r + (req_count - d), req_count)

    def head_peer(d):
        return lax.rem(me_h + d, head_count)

    def head_source(d):
        return lax.rem(me_h + (head_count - d), head_count)

    def remote(src, dst, send, recv, r, h):
        return pltpu.make_async_remote_copy(
            src_ref=src, dst_ref=dst, send_sem=send, recv_sem=recv,
            device_id=(r, h), device_id_type=MESH,
        )

    barrier = pltpu.get_barrier_semaphore()
    for d in range(1, head_count):
        pl.semaphore_signal(barrier, inc=1, device_id=(me_r, head_peer(d)), device_id_type=MESH)
    for d in range(1, req_count):
        pl.semaphore_signal(barrier, inc=1, device_id=(req_peer(d), me_h), device_id_type=MESH)
    small = [
        pltpu.make_async_copy(src, dst, small_sems.at[i])
        for i, (src, dst) in enumerate((
            (lengths_hbm, lengths_ref), (q_hbm, q_ref), (nk_hbm, nk_ref), (nv_hbm, nv_ref),
            (ids_hbm, ids_ref), (rw_hbm, rw_ref), (hid_hbm, hid_ref), (gain_hbm, gain_ref),
            (score_hbm, score_ref),
        ))
    ]
    for load in small:
        load.start()
    caches = [
        [pltpu.make_async_copy(hbm.at[b], buf.at[b], sem.at[b]) for b in range(rows)]
        for hbm, buf, sem in ((k_hbm, k_buf, k_sem), (v_hbm, v_buf, v_sem))
    ]
    for loads in caches:
        for load in loads:
            load.start()
    proj_load = pltpu.make_async_copy(proj_hbm, proj_buf, proj_sem)
    proj_load.start()
    loads = [
        pltpu.make_async_copy(src, dst, weight_sems.at[i])
        for i, (src, dst) in enumerate((
            (eg_hbm.at[0], eg), (eu_hbm.at[0], eu), (sg_hbm, sg), (su_hbm, su),
            (sd_hbm, sd), (ed_hbm.at[0], ed),
        ))
    ]
    for load in loads:
        load.start()

    for load in small:
        load.wait()

    span, width = k_buf.shape[1:]
    scale = HD ** (-0.5)
    group = max(8, width // HD)
    own_head = (
        lax.broadcasted_iota(jnp.int32, (group, width), 0)
        == lax.broadcasted_iota(jnp.int32, (group, width), 1) // HD
    )
    position = lax.broadcasted_iota(jnp.int32, (group, span), 1)
    queries = q_ref[...].astype(jnp.float32)
    own_keys = nk_ref[...].astype(jnp.float32)
    own_values = nv_ref[...].astype(jnp.float32)
    spread = [jnp.where(own_head, queries[b:b + 1, :], 0.0) for b in range(rows)]
    all_scores = []
    for b in range(rows):
        caches[0][b].wait()
        all_scores.append(lax.dot_general(
            spread[b].astype(jnp.bfloat16), k_buf[b], (((1,), (1,)), ((), ())),
            preferred_element_type=jnp.float32,
        ))
    probs = []
    own_probs = []
    for b in range(rows):
        own_score = jnp.sum(spread[b] * own_keys[b:b + 1, :], axis=1, keepdims=True) * scale
        alive = position < lengths_ref[b]
        scores = jnp.where(alive, all_scores[b] * scale, -1e30)
        highest = jnp.maximum(jnp.max(scores, axis=1, keepdims=True), own_score)
        exps = jnp.where(alive, jnp.exp(scores - highest), 0.0)
        own_exp = jnp.exp(own_score - highest)
        norm = jnp.sum(exps, axis=1, keepdims=True) + own_exp
        probs.append((exps / norm).astype(jnp.bfloat16))
        own_probs.append((own_exp / norm).astype(jnp.bfloat16).astype(jnp.float32))

    lane = lax.broadcasted_iota(jnp.int32, (rows, 128), 1)
    table = jnp.zeros((rows, 128), jnp.float32)
    route = rw_ref[...].astype(jnp.float32)
    ids = ids_ref[...].astype(jnp.float32)
    diagonal = (
        lax.broadcasted_iota(jnp.int32, (rows, rows), 0)
        == lax.broadcasted_iota(jnp.int32, (rows, rows), 1)
    )
    lane_value = lane.astype(jnp.float32)
    for k in range(ids.shape[0]):
        chosen = jnp.sum(jnp.where(diagonal, ids[k:k + 1, :], 0.0), axis=1, keepdims=True)
        share = jnp.sum(jnp.where(diagonal, route[k:k + 1, :], 0.0), axis=1, keepdims=True)
        table = table + jnp.where(chosen == lane_value, share, 0.0)
    w_all[me_r] = table
    pl.semaphore_wait(barrier, head_count + req_count - 2)

    def my_cols(h):
        return pl.ds(pl.multiple_of(h * cols, 128), cols)

    sends = []

    def start(copy):
        copy.start()
        sends.append(copy)

    for d in range(1, req_count):
        start(remote(
            w_all.at[me_r], w_all.at[me_r], w_send.at[d], w_recv.at[d], req_peer(d), me_h,
        ))
    for b in range(rows):
        caches[1][b].wait()
        mixed = jnp.dot(probs[b], v_buf[b], preferred_element_type=jnp.float32)
        mixed = mixed + own_probs[b] * own_values[b:b + 1, :]
        attended[b:b + 1, :] = jnp.sum(jnp.where(own_head, mixed, 0.0), axis=0, keepdims=True)
    proj_load.wait()
    part_ref[...] = jnp.dot(
        attended[...].astype(jnp.bfloat16), proj_buf[...], preferred_element_type=jnp.float32
    )
    for d in range(1, head_count):
        start(remote(
            part_ref.at[:, my_cols(head_peer(d))], terms1.at[d], s1.at[d], r1.at[d],
            me_r, head_peer(d),
        ))
    summed = part_ref[:, my_cols(me_h)]
    for d in range(1, head_count):
        remote(
            part_ref.at[:, my_cols(me_h)], terms1.at[d], s1.at[d], r1.at[d], me_r, head_peer(d),
        ).wait_recv()
        summed = summed + terms1[d]
    resid = (hid_ref[:, my_cols(me_h)].astype(jnp.float32) + summed).astype(jnp.bfloat16)
    resid_all[me_h, me_r] = resid

    for d in range(1, req_count):
        block = resid_all.at[me_h, me_r]
        start(remote(block, block, s2.at[d], r2.at[d], req_peer(d), me_h))
    for j in range(req_count):
        block = resid_all.at[me_h, req_source(j)]
        if j > 0:
            remote(block, block, s2.at[j], r2.at[j], req_peer(j), me_h).wait_recv()
        for d in range(1, head_count):
            start(remote(block, block, s3.at[d, j], r3.at[d, j], me_r, head_peer(d)))
    for j in range(req_count):
        for d in range(1, head_count):
            block = resid_all.at[head_source(d), req_source(j)]
            remote(block, block, s3.at[d, j], r3.at[d, j], me_r, head_peer(d)).wait_recv()

    wide = [
        resid_all[h].astype(jnp.float32).reshape(tokens, cols) for h in range(head_count)
    ]
    square = jnp.sum(wide[0] * wide[0], axis=1, keepdims=True)
    for h in range(1, head_count):
        square = square + jnp.sum(wide[h] * wide[h], axis=1, keepdims=True)
    inverse = lax.rsqrt(square / model + EPSILON)
    normed = [
        (wide[h] * inverse * gain_ref[:, h * cols:(h + 1) * cols]).astype(jnp.bfloat16)
        for h in range(head_count)
    ]
    logit = jnp.zeros((tokens, 1), jnp.float32)
    for h in range(head_count):
        logit = logit + jnp.sum(
            normed[h].astype(jnp.float32) * score_ref[:, h * cols:(h + 1) * cols],
            axis=1, keepdims=True,
        )
    gate_scale = 1.0 / (1.0 + jnp.exp(-logit))
    for load in loads:
        load.wait()

    def project_t(weight):
        out = None
        for h in range(head_count):
            term = lax.dot_general(
                normed[h], weight[:, h * cols:(h + 1) * cols], (((1,), (1,)), ((), ())),
                preferred_element_type=jnp.float32,
            )
            out = term if out is None else out + term
        return out

    inner = (silu(project_t(eg)) * project_t(eu)).astype(jnp.bfloat16)
    shared = (silu(project_t(sg)) * project_t(su)).astype(jnp.bfloat16)
    for d in range(1, req_count):
        block = w_all.at[req_source(d)]
        remote(block, block, w_send.at[d], w_recv.at[d], req_peer(d), me_h).wait_recv()
    weights = w_all[...].reshape(tokens, 128)
    wide_lane = lax.broadcasted_iota(jnp.int32, (tokens, 128), 1)
    weight = jnp.sum(jnp.where(wide_lane == me_r, weights, 0.0), axis=1, keepdims=True)

    def column_terms(h):
        part = my_cols(h)
        term = gate_scale * jnp.dot(shared, sd[:, part], preferred_element_type=jnp.float32)
        term = term + weight * jnp.dot(inner, ed[:, part], preferred_element_type=jnp.float32)
        return term.reshape(req_count, rows, cols)

    for d in range(1, head_count):
        send5[d] = column_terms(head_peer(d)).astype(jnp.bfloat16)
        start(remote(send5.at[d], terms5.at[d], s5.at[d], r5.at[d], me_r, head_peer(d)))
    total = column_terms(me_h)
    for d in range(1, head_count):
        remote(
            send5.at[d], terms5.at[d], s5.at[d], r5.at[d], me_r, head_peer(d)
        ).wait_recv()
        total = total + terms5[d].astype(jnp.float32)
    total6[...] = total
    send6[...] = total.astype(jnp.bfloat16)
    for d in range(1, req_count):
        start(remote(
            send6.at[req_peer(d)], terms6.at[d], s6.at[d], r6.at[d], req_peer(d), me_h
        ))
    combined = total6[me_r]
    for d in range(1, req_count):
        remote(
            send6.at[req_peer(d)], terms6.at[d], s6.at[d], r6.at[d], req_peer(d), me_h
        ).wait_recv()
        combined = combined + terms6[d].astype(jnp.float32)
    final[me_h] = (resid.astype(jnp.float32) + combined).astype(jnp.bfloat16)
    for d in range(1, head_count):
        start(remote(
            final.at[me_h], final.at[me_h], s7.at[d], r7.at[d], me_r, head_peer(d)
        ))
    for d in range(1, head_count):
        block = final.at[head_source(d)]
        remote(block, block, s7.at[d], r7.at[d], me_r, head_peer(d)).wait_recv()
    for h in range(head_count):
        out_ref[:, h * cols:(h + 1) * cols] = final[h]
    for copy in sends:
        copy.wait_send()


VMEM_SPEC = pl.BlockSpec(memory_space=pltpu.VMEM)
HBM_SPEC = pl.BlockSpec(memory_space=pltpu.HBM)


def per_device(
    req_count, head_count,
    hidden_in, queries, new_keys, new_values, key_cache, value_cache, lengths, out_proj,
    norm_gain, shared_gate, shared_up, shared_down, shared_score, expert_gate, expert_up,
    expert_down, expert_ids, route_weight,
):
    rows, model = hidden_in.shape
    span, width = key_cache.shape[1:]
    bf16, f32 = jnp.bfloat16, jnp.float32
    dma = pltpu.SemaphoreType.DMA
    cols = model // head_count
    return pl.pallas_call(
        functools.partial(layer_kernel, req_count, head_count),
        out_shape=jax.ShapeDtypeStruct((rows, model), bf16),
        in_specs=[HBM_SPEC] * 18,
        out_specs=VMEM_SPEC,
        scratch_shapes=[
            pltpu.SMEM((rows,), jnp.int32),
            pltpu.VMEM((rows, width), bf16),
            pltpu.VMEM((rows, width), bf16),
            pltpu.VMEM((rows, width), bf16),
            pltpu.VMEM((rows, span, width), bf16),
            pltpu.VMEM((rows, span, width), bf16),
            pltpu.VMEM(out_proj.shape, bf16),
            dma((rows,)), dma((rows,)), dma,
            pltpu.VMEM((rows, width), f32),
            pltpu.VMEM((rows, model), f32),
            pltpu.VMEM((rows, model), bf16),
            pltpu.VMEM((1, model), f32),
            pltpu.VMEM((1, model), f32),
            pltpu.VMEM(expert_ids.shape[::-1], jnp.int32),
            pltpu.VMEM(route_weight.shape[::-1], bf16),
            dma((9,)),
            pltpu.VMEM(shared_gate.shape, bf16),
            pltpu.VMEM(shared_up.shape, bf16),
            pltpu.VMEM(shared_down.shape, bf16),
            pltpu.VMEM(expert_gate.shape[:0:-1], bf16),
            pltpu.VMEM(expert_up.shape[:0:-1], bf16),
            pltpu.VMEM(expert_down.shape[1:], bf16),
            dma((6,)),
            pltpu.VMEM((req_count, rows, 128), f32),
            pltpu.VMEM((head_count, rows, cols), f32),
            pltpu.VMEM((head_count, req_count, rows, cols), bf16),
            pltpu.VMEM((head_count, req_count, rows, cols), bf16),
            pltpu.VMEM((head_count, req_count, rows, cols), bf16),
            pltpu.VMEM((req_count, rows, cols), f32),
            pltpu.VMEM((req_count, rows, cols), bf16),
            pltpu.VMEM((req_count, rows, cols), bf16),
            pltpu.VMEM((head_count, rows, cols), bf16),
            dma((req_count,)), dma((req_count,)),
            dma((head_count,)), dma((head_count,)),
            dma((req_count,)), dma((req_count,)),
            dma((head_count, req_count)), dma((head_count, req_count)),
            dma((head_count,)), dma((head_count,)),
            dma((req_count,)), dma((req_count,)),
            dma((head_count,)), dma((head_count,)),
        ],
        compiler_params=pltpu.CompilerParams(
            vmem_limit_bytes=64 << 20, collective_id=0, has_side_effects=True
        ),
        name="layer",
    )(
        lengths, queries, new_keys, new_values, key_cache, value_cache, out_proj,
        hidden_in, norm_gain.reshape(1, model), shared_score.reshape(1, model),
        expert_ids.T, route_weight.T,
        shared_gate, shared_up, shared_down,
        jnp.swapaxes(expert_gate, 1, 2), jnp.swapaxes(expert_up, 1, 2), expert_down,
    )


def solution(mesh):
    in_specs = (
        P("req", None),
        P("req", "head"),
        P("req", "head"),
        P("req", "head"),
        P("req", None, "head"),
        P("req", None, "head"),
        P("req"),
        P("head", None),
        P(),
        P(("req", "head"), None),
        P(("req", "head"), None),
        P(("req", "head"), None),
        P(),
        P("req", None, "head"),
        P("req", None, "head"),
        P("req", "head", None),
        P("req", None),
        P("req", None),
    )
    body = functools.partial(per_device, mesh.shape["req"], mesh.shape["head"])
    return jax.shard_map(
        body, mesh=mesh, in_specs=in_specs, out_specs=P("req", None), check_vma=False
    )
```

```python
import functools

import jax
import jax.numpy as jnp
from jax import lax
from jax.experimental import pallas as pl
from jax.experimental.pallas import tpu as pltpu
from jax.sharding import PartitionSpec as P

HD = 128
EPSILON = 1e-06
MESH = pl.DeviceIdType.MESH


def silu(x):
    return x / (1.0 + jnp.exp(-x))


def layer_kernel(
    req_count, head_count,
    lengths_hbm, q_hbm, nk_hbm, nv_hbm, k_hbm, v_hbm, proj_hbm,
    hid_hbm, gain_hbm, score_hbm, ids_hbm, rw_hbm,
    sg_hbm, su_hbm, sd_hbm, eg_hbm, eu_hbm, ed_hbm,
    out_ref,
    lengths_ref, q_ref, nk_ref, nv_ref, k_buf, v_buf, proj_buf, k_sem, v_sem, proj_sem,
    attended, part_ref,
    hid_ref, gain_ref, score_ref, ids_ref, rw_ref, small_sems,
    sg, su, sd, eg, eu, ed, weight_sems,
    w_all, terms1, resid_all, send5, terms5, total6, send6, terms6, final,
    w_send, w_recv, s1, r1, s2, r2, s3, r3, s5, r5, s6, r6, s7, r7,
):
    rows, model = hid_ref.shape
    cols = model // head_count
    tokens = req_count * rows
    me_r = lax.axis_index("req")
    me_h = lax.axis_index("head")

    def req_peer(d):
        return lax.rem(me_r + d, req_count)

    def req_source(d):
        return lax.rem(me_r + (req_count - d), req_count)

    def head_peer(d):
        return lax.rem(me_h + d, head_count)

    def head_source(d):
        return lax.rem(me_h + (head_count - d), head_count)

    def remote(src, dst, send, recv, r, h):
        return pltpu.make_async_remote_copy(
            src_ref=src, dst_ref=dst, send_sem=send, recv_sem=recv,
            device_id=(r, h), device_id_type=MESH,
        )

    barrier = pltpu.get_barrier_semaphore()
    for d in range(1, head_count):
        pl.semaphore_signal(barrier, inc=1, device_id=(me_r, head_peer(d)), device_id_type=MESH)
    for d in range(1, req_count):
        pl.semaphore_signal(barrier, inc=1, device_id=(req_peer(d), me_h), device_id_type=MESH)
    small = [
        pltpu.make_async_copy(src, dst, small_sems.at[i])
        for i, (src, dst) in enumerate((
            (lengths_hbm, lengths_ref), (q_hbm, q_ref), (nk_hbm, nk_ref), (nv_hbm, nv_ref),
            (ids_hbm, ids_ref), (rw_hbm, rw_ref), (hid_hbm, hid_ref), (gain_hbm, gain_ref),
            (score_hbm, score_ref),
        ))
    ]
    for load in small:
        load.start()
    caches = [
        [pltpu.make_async_copy(hbm.at[b], buf.at[b], sem.at[b]) for b in range(rows)]
        for hbm, buf, sem in ((k_hbm, k_buf, k_sem), (v_hbm, v_buf, v_sem))
    ]
    for load in caches[0]:
        load.start()
    proj_load = pltpu.make_async_copy(proj_hbm, proj_buf, proj_sem)
    loads = [
        pltpu.make_async_copy(src, dst, weight_sems.at[i])
        for i, (src, dst) in enumerate((
            (eg_hbm.at[0], eg), (eu_hbm.at[0], eu), (sg_hbm, sg), (su_hbm, su),
            (sd_hbm, sd), (ed_hbm.at[0], ed),
        ))
    ]

    for load in small:
        load.wait()

    span, width = k_buf.shape[1:]
    scale = HD ** (-0.5)
    group = max(8, width // HD)
    own_head = (
        lax.broadcasted_iota(jnp.int32, (group, width), 0)
        == lax.broadcasted_iota(jnp.int32, (group, width), 1) // HD
    )
    position = lax.broadcasted_iota(jnp.int32, (group, span), 1)
    queries = q_ref[...].astype(jnp.float32)
    own_keys = nk_ref[...].astype(jnp.float32)
    own_values = nv_ref[...].astype(jnp.float32)
    spread = [jnp.where(own_head, queries[b:b + 1, :], 0.0) for b in range(rows)]
    all_scores = []
    for b in range(rows):
        caches[0][b].wait()
        caches[1][b].start()
        all_scores.append(lax.dot_general(
            spread[b].astype(jnp.bfloat16), k_buf[b], (((1,), (1,)), ((), ())),
            preferred_element_type=jnp.float32,
        ))
    proj_load.start()
    probs = []
    own_probs = []
    for b in range(rows):
        own_score = jnp.sum(spread[b] * own_keys[b:b + 1, :], axis=1, keepdims=True) * scale
        alive = position < lengths_ref[b]
        scores = jnp.where(alive, all_scores[b] * scale, -1e30)
        highest = jnp.maximum(jnp.max(scores, axis=1, keepdims=True), own_score)
        exps = jnp.where(alive, jnp.exp(scores - highest), 0.0)
        own_exp = jnp.exp(own_score - highest)
        norm = jnp.sum(exps, axis=1, keepdims=True) + own_exp
        probs.append((exps / norm).astype(jnp.bfloat16))
        own_probs.append((own_exp / norm).astype(jnp.bfloat16).astype(jnp.float32))

    lane = lax.broadcasted_iota(jnp.int32, (rows, 128), 1)
    table = jnp.zeros((rows, 128), jnp.float32)
    route = rw_ref[...].astype(jnp.float32)
    ids = ids_ref[...].astype(jnp.float32)
    diagonal = (
        lax.broadcasted_iota(jnp.int32, (rows, rows), 0)
        == lax.broadcasted_iota(jnp.int32, (rows, rows), 1)
    )
    lane_value = lane.astype(jnp.float32)
    for k in range(ids.shape[0]):
        chosen = jnp.sum(jnp.where(diagonal, ids[k:k + 1, :], 0.0), axis=1, keepdims=True)
        share = jnp.sum(jnp.where(diagonal, route[k:k + 1, :], 0.0), axis=1, keepdims=True)
        table = table + jnp.where(chosen == lane_value, share, 0.0)
    w_all[me_r] = table
    pl.semaphore_wait(barrier, head_count + req_count - 2)

    def my_cols(h):
        return pl.ds(pl.multiple_of(h * cols, 128), cols)

    sends = []

    def start(copy):
        copy.start()
        sends.append(copy)

    for d in range(1, req_count):
        start(remote(
            w_all.at[me_r], w_all.at[me_r], w_send.at[d], w_recv.at[d], req_peer(d), me_h,
        ))
    for b in range(rows):
        caches[1][b].wait()
        mixed = jnp.dot(probs[b], v_buf[b], preferred_element_type=jnp.float32)
        mixed = mixed + own_probs[b] * own_values[b:b + 1, :]
        attended[b:b + 1, :] = jnp.sum(jnp.where(own_head, mixed, 0.0), axis=0, keepdims=True)
    proj_load.wait()
    part_ref[...] = jnp.dot(
        attended[...].astype(jnp.bfloat16), proj_buf[...], preferred_element_type=jnp.float32
    )
    for d in range(1, head_count):
        start(remote(
            part_ref.at[:, my_cols(head_peer(d))], terms1.at[d], s1.at[d], r1.at[d],
            me_r, head_peer(d),
        ))
    for load in loads:
        load.start()
    summed = part_ref[:, my_cols(me_h)]
    for d in range(1, head_count):
        remote(
            part_ref.at[:, my_cols(me_h)], terms1.at[d], s1.at[d], r1.at[d], me_r, head_peer(d),
        ).wait_recv()
        summed = summed + terms1[d]
    resid = (hid_ref[:, my_cols(me_h)].astype(jnp.float32) + summed).astype(jnp.bfloat16)
    resid_all[me_h, me_r] = resid

    for d in range(1, req_count):
        block = resid_all.at[me_h, me_r]
        start(remote(block, block, s2.at[d], r2.at[d], req_peer(d), me_h))
    for j in range(req_count):
        block = resid_all.at[me_h, req_source(j)]
        if j > 0:
            remote(block, block, s2.at[j], r2.at[j], req_peer(j), me_h).wait_recv()
        for d in range(1, head_count):
            start(remote(block, block, s3.at[d, j], r3.at[d, j], me_r, head_peer(d)))
    for j in range(req_count):
        for d in range(1, head_count):
            block = resid_all.at[head_source(d), req_source(j)]
            remote(block, block, s3.at[d, j], r3.at[d, j], me_r, head_peer(d)).wait_recv()

    wide = [
        resid_all[h].astype(jnp.float32).reshape(tokens, cols) for h in range(head_count)
    ]
    square = jnp.sum(wide[0] * wide[0], axis=1, keepdims=True)
    for h in range(1, head_count):
        square = square + jnp.sum(wide[h] * wide[h], axis=1, keepdims=True)
    inverse = lax.rsqrt(square / model + EPSILON)
    normed = [
        (wide[h] * inverse * gain_ref[:, h * cols:(h + 1) * cols]).astype(jnp.bfloat16)
        for h in range(head_count)
    ]
    logit = jnp.zeros((tokens, 1), jnp.float32)
    for h in range(head_count):
        logit = logit + jnp.sum(
            normed[h].astype(jnp.float32) * score_ref[:, h * cols:(h + 1) * cols],
            axis=1, keepdims=True,
        )
    gate_scale = 1.0 / (1.0 + jnp.exp(-logit))
    for load in loads:
        load.wait()

    def project_t(weight):
        out = None
        for h in range(head_count):
            term = lax.dot_general(
                normed[h], weight[:, h * cols:(h + 1) * cols], (((1,), (1,)), ((), ())),
                preferred_element_type=jnp.float32,
            )
            out = term if out is None else out + term
        return out

    inner = (silu(project_t(eg)) * project_t(eu)).astype(jnp.bfloat16)
    shared = (silu(project_t(sg)) * project_t(su)).astype(jnp.bfloat16)
    for d in range(1, req_count):
        block = w_all.at[req_source(d)]
        remote(block, block, w_send.at[d], w_recv.at[d], req_peer(d), me_h).wait_recv()
    weights = w_all[...].reshape(tokens, 128)
    wide_lane = lax.broadcasted_iota(jnp.int32, (tokens, 128), 1)
    weight = jnp.sum(jnp.where(wide_lane == me_r, weights, 0.0), axis=1, keepdims=True)

    def column_terms(h):
        part = my_cols(h)
        term = gate_scale * jnp.dot(shared, sd[:, part], preferred_element_type=jnp.float32)
        term = term + weight * jnp.dot(inner, ed[:, part], preferred_element_type=jnp.float32)
        return term.reshape(req_count, rows, cols)

    for d in range(1, head_count):
        send5[d] = column_terms(head_peer(d)).astype(jnp.bfloat16)
        start(remote(send5.at[d], terms5.at[d], s5.at[d], r5.at[d], me_r, head_peer(d)))
    total = column_terms(me_h)
    for d in range(1, head_count):
        remote(
            send5.at[d], terms5.at[d], s5.at[d], r5.at[d], me_r, head_peer(d)
        ).wait_recv()
        total = total + terms5[d].astype(jnp.float32)
    total6[...] = total
    send6[...] = total.astype(jnp.bfloat16)
    for d in range(1, req_count):
        start(remote(
            send6.at[req_peer(d)], terms6.at[d], s6.at[d], r6.at[d], req_peer(d), me_h
        ))
    combined = total6[me_r]
    for d in range(1, req_count):
        remote(
            send6.at[req_peer(d)], terms6.at[d], s6.at[d], r6.at[d], req_peer(d), me_h
        ).wait_recv()
        combined = combined + terms6[d].astype(jnp.float32)
    final[me_h] = (resid.astype(jnp.float32) + combined).astype(jnp.bfloat16)
    for d in range(1, head_count):
        start(remote(
            final.at[me_h], final.at[me_h], s7.at[d], r7.at[d], me_r, head_peer(d)
        ))
    for d in range(1, head_count):
        block = final.at[head_source(d)]
        remote(block, block, s7.at[d], r7.at[d], me_r, head_peer(d)).wait_recv()
    for h in range(head_count):
        out_ref[:, h * cols:(h + 1) * cols] = final[h]
    for copy in sends:
        copy.wait_send()


VMEM_SPEC = pl.BlockSpec(memory_space=pltpu.VMEM)
HBM_SPEC = pl.BlockSpec(memory_space=pltpu.HBM)


def per_device(
    req_count, head_count,
    hidden_in, queries, new_keys, new_values, key_cache, value_cache, lengths, out_proj,
    norm_gain, shared_gate, shared_up, shared_down, shared_score, expert_gate, expert_up,
    expert_down, expert_ids, route_weight,
):
    rows, model = hidden_in.shape
    span, width = key_cache.shape[1:]
    bf16, f32 = jnp.bfloat16, jnp.float32
    dma = pltpu.SemaphoreType.DMA
    cols = model // head_count
    return pl.pallas_call(
        functools.partial(layer_kernel, req_count, head_count),
        out_shape=jax.ShapeDtypeStruct((rows, model), bf16),
        in_specs=[HBM_SPEC] * 18,
        out_specs=VMEM_SPEC,
        scratch_shapes=[
            pltpu.SMEM((rows,), jnp.int32),
            pltpu.VMEM((rows, width), bf16),
            pltpu.VMEM((rows, width), bf16),
            pltpu.VMEM((rows, width), bf16),
            pltpu.VMEM((rows, span, width), bf16),
            pltpu.VMEM((rows, span, width), bf16),
            pltpu.VMEM(out_proj.shape, bf16),
            dma((rows,)), dma((rows,)), dma,
            pltpu.VMEM((rows, width), f32),
            pltpu.VMEM((rows, model), f32),
            pltpu.VMEM((rows, model), bf16),
            pltpu.VMEM((1, model), f32),
            pltpu.VMEM((1, model), f32),
            pltpu.VMEM(expert_ids.shape[::-1], jnp.int32),
            pltpu.VMEM(route_weight.shape[::-1], bf16),
            dma((9,)),
            pltpu.VMEM(shared_gate.shape, bf16),
            pltpu.VMEM(shared_up.shape, bf16),
            pltpu.VMEM(shared_down.shape, bf16),
            pltpu.VMEM(expert_gate.shape[:0:-1], bf16),
            pltpu.VMEM(expert_up.shape[:0:-1], bf16),
            pltpu.VMEM(expert_down.shape[1:], bf16),
            dma((6,)),
            pltpu.VMEM((req_count, rows, 128), f32),
            pltpu.VMEM((head_count, rows, cols), f32),
            pltpu.VMEM((head_count, req_count, rows, cols), bf16),
            pltpu.VMEM((head_count, req_count, rows, cols), bf16),
            pltpu.VMEM((head_count, req_count, rows, cols), bf16),
            pltpu.VMEM((req_count, rows, cols), f32),
            pltpu.VMEM((req_count, rows, cols), bf16),
            pltpu.VMEM((req_count, rows, cols), bf16),
            pltpu.VMEM((head_count, rows, cols), bf16),
            dma((req_count,)), dma((req_count,)),
            dma((head_count,)), dma((head_count,)),
            dma((req_count,)), dma((req_count,)),
            dma((head_count, req_count)), dma((head_count, req_count)),
            dma((head_count,)), dma((head_count,)),
            dma((req_count,)), dma((req_count,)),
            dma((head_count,)), dma((head_count,)),
        ],
        compiler_params=pltpu.CompilerParams(
            vmem_limit_bytes=64 << 20, collective_id=0, has_side_effects=True
        ),
        name="layer",
    )(
        lengths, queries, new_keys, new_values, key_cache, value_cache, out_proj,
        hidden_in, norm_gain.reshape(1, model), shared_score.reshape(1, model),
        expert_ids.T, route_weight.T,
        shared_gate, shared_up, shared_down,
        jnp.swapaxes(expert_gate, 1, 2), jnp.swapaxes(expert_up, 1, 2), expert_down,
    )


def solution(mesh):
    in_specs = (
        P("req", None),
        P("req", "head"),
        P("req", "head"),
        P("req", "head"),
        P("req", None, "head"),
        P("req", None, "head"),
        P("req"),
        P("head", None),
        P(),
        P(("req", "head"), None),
        P(("req", "head"), None),
        P(("req", "head"), None),
        P(),
        P("req", None, "head"),
        P("req", None, "head"),
        P("req", "head", None),
        P("req", None),
        P("req", None),
    )
    body = functools.partial(per_device, mesh.shape["req"], mesh.shape["head"])
    return jax.shard_map(
        body, mesh=mesh, in_specs=in_specs, out_specs=P("req", None), check_vma=False
    )
```
